32 devices in a mesh: parts: 2 (over y), pair: 4 (over x, core), sub: 4 (over z).
Axes of the slice: x: 2, y: 2, z: 4, core: 2. Of those that a mesh axis runs over, the one named last changes fastest.
Arguments:
- features: bfloat16 [64, 1024, 256], P(('parts', 'pair'), 'sub'), parts along dimension 0, may hold values from -7 to 7
- counts: int32 [64], P('parts'), parts along dimension 0, may hold values from 256 to 1024
- pair_table: int32 [8, 4, 2], P('parts'), parts along dimension 0, may hold values from -1 to 31, as said below
- w_qk: bfloat16 [256, 256], replicated, may hold values from -0.75 to 0.75
- w_value: bfloat16 [256, 256], replicated, may hold values from -0.375 to 0.375
- w_out: bfloat16 [256, 256], replicated, may hold values from -1.5 to 1.5
- w_merge_in: bfloat16 [512, 512], replicated, may hold values from -0.25 to 0.25
- w_merge_out: bfloat16 [512, 256], replicated, may hold values from -0.25 to 0.25
Outputs:
- updated: bfloat16 [64, 1024, 256], P(('parts', 'pair'), 'sub'), parts along dimension 0
The draws below stay inside these ranges and needn't reach their ends.
There are 2 independent parts, one for each index of `parts`. The reference program is written for one: setup_inputs(seed, part) draws one part's arguments, and reference() takes and returns one part's arrays. A program takes and returns all parts, laid end to end along the dimension named above; an argument that names none is the same for every part. Nothing has to cross between parts.
Inputs may be any that keep to these rules, and one draw needn't show every extreme that they name: `pair_table`: row g lists the pairs owned by index g of pair, one slot per index of sub; -1 in both entries marks an empty slot. A live slot names two images of different groups, image i belonging to group i // 8. Over the live slots of one owner, at most 2 named images (counted with repetition) belong to any one group; some owner has all 4 slots live and reaches that bound for every group.
All inputs are finite; a program needn't handle non-finite values.
Results may differ from the reference program's by a relative error of at most 0.0067.
Values may be sent and summed in bfloat16 or wider, within the bound.
A program may use at most 64 MiB of HBM per device.

```python
import jax
import jax.numpy as jnp
from jax import lax

D = 256
HEADS = 4
KP = 1024
IMG_GRP = 8
GROUPS = 4
SLOTS = 4
IMAGES = 32
MERGE = 512


def pair_layout(key):
    base_load = 5 * SLOTS // 8
    group_order = jax.random.permutation(jax.random.fold_in(key, 101), GROUPS)
    extra_load = jax.random.randint(jax.random.fold_in(key, 102), (GROUPS // 2,), 0, SLOTS - base_load + 1)
    extra_load = extra_load.at[0].set(SLOTS - base_load)
    group_load = jnp.zeros((GROUPS,), jnp.int32)
    group_load = group_load.at[group_order[0::2]].set(base_load + extra_load)
    group_load = group_load.at[group_order[1::2]].set(base_load - extra_load)
    source_perm = jax.vmap(lambda sub_key: jax.random.permutation(sub_key, GROUPS))(jax.random.split(jax.random.fold_in(key, 103), GROUPS))
    position_src = jnp.take(source_perm, jnp.arange(2 * SLOTS) % GROUPS, axis=1)
    local_index = jax.random.randint(jax.random.fold_in(key, 104), (GROUPS, 2 * SLOTS), 0, IMG_GRP)
    image_id = (position_src * IMG_GRP + local_index).reshape(GROUPS, SLOTS, 2)
    slot_live = jnp.arange(SLOTS)[None, :] < group_load[:, None]
    image_id = jnp.where(slot_live[:, :, None], image_id, -1)
    slot_perm = jax.vmap(lambda sub_key: jax.random.permutation(sub_key, SLOTS))(jax.random.split(jax.random.fold_in(key, 105), GROUPS))
    slot_perm = jnp.repeat(slot_perm[:, :, None], 2, axis=2)
    image_id = jnp.take_along_axis(image_id, slot_perm, axis=1)
    return image_id.astype(jnp.int32)


def draw_pair_table(key, part):
    return pair_layout(key)


def draw_features(key, part):
    shape = (IMAGES, KP, D)
    base_vals = jnp.clip(jax.random.normal(jax.random.fold_in(key, 1), shape, jnp.float32), -4.0, 4.0)
    return base_vals.astype(jnp.bfloat16)


def set_ends(array, key, least, largest):
    extent = array.shape
    place = [jax.random.randint(jax.random.fold_in(key, axis), (), 0, extent[axis]) for axis in range(len(extent))]
    array = array.at[tuple(place)].set(least)
    longest = extent.index(max(extent))
    place[longest] = (place[longest] + 1) % extent[longest]
    return array.at[tuple(place)].set(largest)


def normal_values(key, dims, spread, bound, held_as=jnp.bfloat16):
    return jnp.clip(spread * jax.random.normal(key, dims, jnp.float32), -bound, bound).astype(held_as)


def setup_inputs(seed: int = 0, part: int = 0) -> dict:
    streams_of = jax.random.split(jax.random.key(seed), 9)
    part_keys = jax.random.split(jax.random.fold_in(streams_of[8], part), 9)
    return {
        "features": draw_features(jax.random.fold_in(jax.random.fold_in(streams_of[8], part), 71), part),
        "counts": set_ends(jax.random.randint(part_keys[1], (IMAGES,), KP // 4, KP + 1), jax.random.fold_in(part_keys[1], 1), KP // 4, KP).astype(jnp.int32),
        "pair_table": draw_pair_table(jax.random.fold_in(jax.random.fold_in(streams_of[8], part), 71), part),
        "w_qk": normal_values(streams_of[3], (D, D), (D // 4) ** -0.5, 0.75),
        "w_value": normal_values(streams_of[4], (D, D), D ** -0.5, 0.375),
        "w_out": normal_values(streams_of[5], (D, D), (D // 16) ** -0.5, 1.5),
        "w_merge_in": normal_values(streams_of[6], (MERGE, MERGE), MERGE ** -0.5, 0.25),
        "w_merge_out": normal_values(streams_of[7], (MERGE, D), MERGE ** -0.5, 0.25),
    }


ln_eps = 1e-05

def layer_norm(hidden):
    center = lax.optimization_barrier(jnp.mean(hidden, axis=-1, keepdims=True))
    centered = hidden - center
    variance = lax.optimization_barrier(jnp.mean(centered * centered, axis=-1, keepdims=True))
    return centered * lax.rsqrt(variance + ln_eps)

def pair_messages(left_feats, right_feats, left_count, right_count, w_qk, w_value, head_count):
    points = left_feats.shape[0]
    model_width = left_feats.shape[1]
    head_dim = model_width // head_count
    stacked = jnp.concatenate([left_feats, right_feats], axis=0)
    query_key = jnp.dot(stacked, w_qk, preferred_element_type=jnp.float32).astype(jnp.bfloat16)
    values = jnp.dot(stacked, w_value, preferred_element_type=jnp.float32).astype(jnp.bfloat16)
    row_ids = lax.broadcasted_iota(jnp.int32, (points, 1), 0)
    col_ids = lax.broadcasted_iota(jnp.int32, (1, points), 1)
    col_valid = col_ids < right_count
    row_valid = row_ids < left_count
    score_scale = head_dim ** (-0.5)
    to_left = []
    to_right = []
    for head_index in range(head_count):
        head_lo = head_index * head_dim
        q_left = query_key[:points, head_lo:head_lo + head_dim]
        q_right = query_key[points:, head_lo:head_lo + head_dim]
        v_left = values[:points, head_lo:head_lo + head_dim]
        v_right = values[points:, head_lo:head_lo + head_dim]
        scores = lax.dot_general(q_left, q_right, (((1,), (1,)), ((), ())), preferred_element_type=jnp.float32) * score_scale
        masked = jnp.where(col_valid, scores, -jnp.inf)
        row_top = lax.optimization_barrier(jnp.max(masked, axis=1, keepdims=True))
        row_exp = jnp.exp(masked - row_top)
        row_total = lax.optimization_barrier(jnp.sum(row_exp, axis=1, keepdims=True))
        to_left.append(jnp.dot(row_exp.astype(jnp.bfloat16), v_right, preferred_element_type=jnp.float32) / row_total)
        col_masked = jnp.where(row_valid, scores, -jnp.inf)
        col_top = lax.optimization_barrier(jnp.max(col_masked, axis=0, keepdims=True))
        col_exp = jnp.exp(col_masked - col_top)
        col_total = lax.optimization_barrier(jnp.sum(col_exp, axis=0, keepdims=True))
        summed = lax.dot_general(col_exp.astype(jnp.bfloat16), v_left, (((0,), (0,)), ((), ())), preferred_element_type=jnp.float32)
        to_right.append(summed / col_total.reshape(points, 1))
    return (jnp.concatenate(to_left, axis=1).astype(jnp.bfloat16), jnp.concatenate(to_right, axis=1).astype(jnp.bfloat16))

def reference(features, counts, pair_table, w_qk, w_value, w_out, w_merge_in, w_merge_out):
    images, points, model_width = features.shape
    slot_list = pair_table.reshape(-1, 2).astype(jnp.int32)

    def add_slot(msg_total, slot):
        left_id = jnp.maximum(slot[0], 0).astype(jnp.int32)
        right_id = jnp.maximum(slot[1], 0).astype(jnp.int32)

        def work(carried):
            left_feats = lax.dynamic_index_in_dim(features, left_id, 0, keepdims=False)
            right_feats = lax.dynamic_index_in_dim(features, right_id, 0, keepdims=False)
            left_count = lax.dynamic_index_in_dim(counts, left_id, 0, keepdims=False)
            right_count = lax.dynamic_index_in_dim(counts, right_id, 0, keepdims=False)
            to_left, to_right = pair_messages(left_feats, right_feats, left_count, right_count, w_qk, w_value, HEADS)
            carried = carried.at[left_id].add(to_left.astype(jnp.float32))
            carried = carried.at[right_id].add(to_right.astype(jnp.float32))
            return carried
        msg_total = lax.cond(slot[0] >= 0, work, lambda carried: carried, msg_total)
        return (msg_total, None)
    msg_total, _ = lax.scan(add_slot, jnp.zeros((images, points, model_width), jnp.float32), slot_list)
    image_ids = jnp.arange(images).astype(jnp.int32)
    use_count = lax.optimization_barrier(jnp.sum((slot_list.reshape(1, -1) == image_ids[:, None]).astype(jnp.int32), axis=1))
    divisor = jnp.maximum(use_count, 1).astype(jnp.float32)
    mean_msg = (msg_total / divisor[:, None, None]).astype(jnp.bfloat16)
    own_rows = features.reshape(-1, model_width)
    lifted = jnp.dot(mean_msg.reshape(-1, model_width), w_out, preferred_element_type=jnp.float32).astype(jnp.bfloat16)
    hidden = jnp.dot(own_rows, w_merge_in[:model_width], preferred_element_type=jnp.float32)
    hidden = hidden + jnp.dot(lifted, w_merge_in[model_width:], preferred_element_type=jnp.float32)
    active = jax.nn.gelu(layer_norm(hidden), approximate=False).astype(jnp.bfloat16)
    updated = own_rows.astype(jnp.float32) + jnp.dot(active, w_merge_out, preferred_element_type=jnp.float32)
    return updated.astype(jnp.bfloat16).reshape(images, points, model_width)
```

```python
import functools

import jax
import jax.numpy as jnp
from jax import lax
from jax.experimental import pallas as pl
from jax.experimental.pallas import tpu as pltpu
from jax.sharding import PartitionSpec as P

HEADS = 4
SLAB = 128
CHUNKS = 2
MESH = pl.DeviceIdType.MESH

ln_eps = 1e-05


def partner(me, step, n):
    if n & (n - 1):
        return lax.rem(me + step, n)
    peer = 0
    bit = 1
    while bit < n:
        mine = (me // bit) % 2
        peer = peer + ((mine + (step // bit) % 2) % 2) * bit
        bit *= 2
    return peer


def source(me, step, n):
    if n & (n - 1):
        return lax.rem(me + n - step, n)
    return partner(me, step, n)


def exchange_kernel(
    dims, idx_ref, feat_ref, wqk_ref, wv_ref, home_ref, *scratch
):
    n_pair, n_sub, per_src, chunks, slabs, head_dim, tile = dims
    img_grp, kp, width = feat_ref.shape
    positions = 2 * n_sub
    sources = n_pair * per_src
    points = n_sub * kp
    scratch = list(scratch)
    send1 = scratch.pop(0)
    send2 = scratch.pop(0)
    rows_in = scratch.pop(0)
    qk = scratch.pop(0)
    vx = scratch.pop(0)
    msg = scratch.pop(0)
    hsend = scratch.pop(0)
    arrived = [scratch.pop(0) for _ in range(chunks)]
    returned = [scratch.pop(0) for _ in range(slabs)]
    s1, r1, s2, r2, s3, r3, s4, r4 = scratch

    me_pair = lax.axis_index("pair")
    me_sub = lax.axis_index("sub")
    part = kp // chunks

    barrier = pltpu.get_barrier_semaphore()
    for step in range(1, n_pair):
        pl.semaphore_signal(
            barrier, inc=1, device_id={"pair": partner(me_pair, step, n_pair)}, device_id_type=MESH
        )
    for step in range(1, n_sub):
        pl.semaphore_signal(
            barrier, inc=1, device_id={"sub": partner(me_sub, step, n_sub)}, device_id_type=MESH
        )
    pl.semaphore_wait(barrier, n_pair + n_sub - 2)

    waits = []
    pair_steps = list(range(n_pair - 1, 0, -1))
    sub_steps = list(range(n_sub - 1, 0, -1))

    phase1 = {}
    for c in range(chunks):
        rows = pl.ds(c * part, part)
        for step in pair_steps:
            peer = partner(me_pair, step, n_pair)
            for r in range(per_src):
                send1[step, r, rows, :] = feat_ref[idx_ref[peer * per_src + r], rows, :]
            copy = pltpu.make_async_remote_copy(
                src_ref=send1.at[step, :, rows, :],
                dst_ref=arrived[c].at[pl.ds(me_pair * per_src, per_src)],
                send_sem=s1.at[step, c],
                recv_sem=r1.at[step, c],
                device_id={"pair": peer},
                device_id_type=MESH,
            )
            copy.start()
            phase1[c, step] = copy
            waits.append(copy)
    for c in range(chunks):
        rows = pl.ds(c * part, part)
        for r in range(per_src):
            arrived[c][me_pair * per_src + r] = feat_ref[idx_ref[me_pair * per_src + r], rows, :]

    phase2 = {}
    for c in range(chunks):
        rows = pl.ds(c * part, part)
        for step in pair_steps:
            phase1[c, step].wait_recv()
        for step in sub_steps:
            peer = partner(me_sub, step, n_sub)
            for side in range(2):
                send2[step, side, rows, :] = arrived[c][idx_ref[sources + 2 * peer + side]]
            copy = pltpu.make_async_remote_copy(
                src_ref=send2.at[step, :, rows, :],
                dst_ref=rows_in.at[me_sub, :, rows, :],
                send_sem=s2.at[step, c],
                recv_sem=r2.at[step, c],
                device_id={"sub": peer},
                device_id_type=MESH,
            )
            copy.start()
            phase2[c, step] = copy
            waits.append(copy)
        for side in range(2):
            rows_in[me_sub, side, rows, :] = arrived[c][idx_ref[sources + 2 * me_sub + side]]

    ones = jnp.ones((kp, SLAB), jnp.bfloat16)

    def project(owner):
        for side in range(2):
            x = rows_in[owner, side]
            where = pl.ds(owner * kp, kp)
            q = jnp.dot(x, wqk_ref[...], preferred_element_type=jnp.float32)
            qk[side, where, :] = q.astype(jnp.bfloat16)
            v = jnp.dot(x, wv_ref[...], preferred_element_type=jnp.float32).astype(jnp.bfloat16)
            for slab in range(slabs):
                vx[side, slab, where, :SLAB] = v[:, slab * SLAB : (slab + 1) * SLAB]
                vx[side, slab, where, SLAB:] = ones

    project(me_sub)
    for step in reversed(sub_steps):
        for c in range(chunks):
            phase2[c, step].wait_recv()
        project(source(me_sub, step, n_sub))

    scale = head_dim ** (-0.5)
    in_slab = SLAB // head_dim
    tile_lane = lax.broadcasted_iota(jnp.int32, (tile, SLAB), 1) // head_dim
    col_ids = lax.broadcasted_iota(jnp.int32, (1, points), 1)
    base = sources + positions + sources

    def attend(side, slab):
        other = 1 - side
        valid = col_ids < idx_ref[base + other]
        columns = slice(slab * SLAB, (slab + 1) * SLAB)

        def body(t, carry):
            start = pl.multiple_of(t * tile, tile)
            q = qk[side, pl.ds(start, tile), columns] * jnp.asarray(scale, jnp.bfloat16)
            out = jnp.zeros((tile, SLAB), jnp.float32)
            for head in range(in_slab):
                mine = tile_lane == head
                qh = jnp.where(mine, q, jnp.zeros_like(q))
                sim = lax.dot_general(
                    qh,
                    qk[other, :, columns],
                    (((1,), (1,)), ((), ())),
                    preferred_element_type=jnp.float32,
                )
                sim = jnp.where(valid, sim, -jnp.inf)
                top = jnp.max(sim, axis=1, keepdims=True)
                weight = jnp.exp(sim - top).astype(jnp.bfloat16)
                both = jnp.dot(weight, vx[other, slab], preferred_element_type=jnp.float32)
                out = jnp.where(mine, both[:, :SLAB] / both[:, SLAB:], out)
            msg[slab, side, pl.ds(start, tile), :] = out.astype(jnp.bfloat16)
            return carry

        lax.fori_loop(0, points // tile, body, 0)

    phase3 = {}
    phase4 = {}

    def give_back(side, slab):
        for step in sub_steps:
            peer = partner(me_sub, step, n_sub)
            copy = pltpu.make_async_remote_copy(
                src_ref=msg.at[slab, side, pl.ds(peer * kp, kp), :],
                dst_ref=returned[slab].at[2 * me_sub + side],
                send_sem=s3.at[step, slab, side],
                recv_sem=r3.at[step, slab, side],
                device_id={"sub": peer},
                device_id_type=MESH,
            )
            copy.start()
            phase3[slab, side, step] = copy
            waits.append(copy)
        returned[slab][2 * me_sub + side] = msg[slab, side, pl.ds(me_sub * kp, kp), :]

    def send_home(slab):
        for side in range(2):
            for step in sub_steps:
                phase3[slab, side, step].wait_recv()
        first = sources + positions
        for step in pair_steps:
            peer = partner(me_pair, step, n_pair)
            for r in range(per_src):
                hsend[slab, step, r] = returned[slab][idx_ref[first + peer * per_src + r]]
            copy = pltpu.make_async_remote_copy(
                src_ref=hsend.at[slab, step],
                dst_ref=home_ref.at[slab, pl.ds(me_pair * per_src, per_src)],
                send_sem=s4.at[step, slab],
                recv_sem=r4.at[step, slab],
                device_id={"pair": peer},
                device_id_type=MESH,
            )
            copy.start()
            phase4[slab, step] = copy
            waits.append(copy)
        for r in range(per_src):
            home_ref[slab, me_pair * per_src + r] = returned[slab][
                idx_ref[first + me_pair * per_src + r]
            ]

    for slab in range(slabs):
        for side in range(2):
            attend(side, slab)
            give_back(side, slab)
    for slab in range(slabs):
        send_home(slab)
    for copy in phase4.values():
        copy.wait_recv()
    for copy in waits:
        copy.wait_send()


def erf(x):
    x = jnp.clip(x, -3.832506856900711, 3.832506856900711)
    y = x * x
    top = jnp.float32(0.00022905065861350646)
    for c in (0.0034082910107109506, 0.050955695062380861, 0.18520832239976145, 1.128379143519084):
        top = top * y + jnp.float32(c)
    low = jnp.float32(-1.1791602954361697e-7)
    for c in (0.000023547966471313185, 0.0010179625278914885, 0.014070470171167667, 0.11098505178285362, 0.49746925110067538, 1.0):
        low = low * y + jnp.float32(c)
    return x * top / low


def update_kernel(dims, weight_ref, feat_ref, home_ref, wout_ref, wmi_ref, wmo_ref, out_ref):
    sources, slabs = dims
    image = pl.program_id(0)
    kp, width = out_ref.shape
    parts = []
    for slab in range(slabs):
        total = jnp.zeros((kp, SLAB), jnp.float32)
        for s in range(sources):
            total = total + home_ref[slab, s].astype(jnp.float32) * weight_ref[image, s]
        parts.append(total)
    mean = (jnp.concatenate(parts, axis=1) / weight_ref[image, sources]).astype(jnp.bfloat16)
    lifted = jnp.dot(mean, wout_ref[...], preferred_element_type=jnp.float32).astype(jnp.bfloat16)
    feat = feat_ref[...]
    hidden = jnp.dot(feat, wmi_ref[:width], preferred_element_type=jnp.float32)
    hidden = hidden + jnp.dot(lifted, wmi_ref[width:], preferred_element_type=jnp.float32)
    center = jnp.mean(hidden, axis=-1, keepdims=True)
    centered = hidden - center
    variance = jnp.mean(centered * centered, axis=-1, keepdims=True)
    normed = centered * lax.rsqrt(variance + ln_eps)
    active = (0.5 * normed * (1.0 + erf(normed * (0.5**0.5)))).astype(jnp.bfloat16)
    out = feat.astype(jnp.float32) + jnp.dot(
        active, wmo_ref[...], preferred_element_type=jnp.float32
    )
    out_ref[...] = out.astype(jnp.bfloat16)


def local(features, counts, pair_table, w_qk, w_value, w_out, w_merge_in, w_merge_out):
    n_pair = lax.axis_size("pair")
    n_sub = lax.axis_size("sub")
    me_group = lax.axis_index("pair")
    me_sub = lax.axis_index("sub")
    img_grp, kp, width = features.shape
    per_src = 2 * n_sub // n_pair
    positions = 2 * n_sub
    sources = n_pair * per_src
    slabs = width // SLAB
    head_dim = width // HEADS
    points = n_sub * kp

    table = pair_table.reshape(n_pair, positions)
    live = table >= 0
    group = jnp.where(live, table // img_grp, -1)
    place = jnp.arange(positions, dtype=jnp.int32)
    earlier = place[None, None, :] < place[None, :, None]
    rank = jnp.sum(
        ((group[:, None, :] == group[:, :, None]) & earlier).astype(jnp.int32), axis=2
    )
    slot_ids = jnp.arange(per_src, dtype=jnp.int32)
    match = (group == me_group)[:, None, :] & (rank[:, None, :] == slot_ids[None, :, None])
    send_local = jnp.sum(
        jnp.where(match, table[:, None, :] - me_group * img_grp, 0), axis=2
    ).reshape(-1)
    send_ok = jnp.any(match, axis=2).reshape(-1)
    mine = lax.dynamic_index_in_dim(table, me_group, 0, keepdims=False)
    my_group = lax.dynamic_index_in_dim(group, me_group, 0, keepdims=False)
    my_rank = lax.dynamic_index_in_dim(rank, me_group, 0, keepdims=False)
    pick = jnp.where(mine >= 0, my_group * per_src + my_rank, 0)
    flat_ids = jnp.arange(sources, dtype=jnp.int32)
    back = jnp.sum(
        jnp.where(
            (pick[None, :] == flat_ids[:, None]) & (mine >= 0)[None, :], place[None, :], 0
        ),
        axis=1,
    )
    slot = jnp.maximum(lax.dynamic_slice_in_dim(mine, 2 * me_sub, 2), 0)
    slot_counts = jnp.take(counts, slot)
    index = jnp.concatenate([send_local, pick, back, slot_counts]).astype(jnp.int32)
    local_ids = jnp.arange(img_grp, dtype=jnp.int32)
    hot = ((send_local[None, :] == local_ids[:, None]) & send_ok[None, :]).astype(jnp.float32)
    uses = jnp.maximum(jnp.sum(hot, axis=1, keepdims=True), 1.0)
    weights = jnp.concatenate([hot, uses], axis=1)

    tile = min(256, points)
    bf = jnp.bfloat16
    chunks = CHUNKS
    dma = pltpu.SemaphoreType.DMA
    vmem = pl.BlockSpec(memory_space=pltpu.VMEM)
    smem = pl.BlockSpec(memory_space=pltpu.SMEM)
    dims = (n_pair, n_sub, per_src, chunks, slabs, head_dim, tile)
    home = pl.pallas_call(
        functools.partial(exchange_kernel, dims),
        out_shape=jax.ShapeDtypeStruct((slabs, sources, kp, SLAB), bf),
        in_specs=[smem, vmem, vmem, vmem],
        out_specs=vmem,
        scratch_shapes=[
            pltpu.VMEM((n_pair, per_src, kp, width), bf),
            pltpu.VMEM((n_sub, 2, kp, width), bf),
            pltpu.VMEM((n_sub, 2, kp, width), bf),
            pltpu.VMEM((2, points, width), bf),
            pltpu.VMEM((2, slabs, points, 2 * SLAB), bf),
            pltpu.VMEM((slabs, 2, points, SLAB), bf),
            pltpu.VMEM((slabs, n_pair, per_src, kp, SLAB), bf),
        ]
        + [pltpu.VMEM((sources, kp // chunks, width), bf) for _ in range(chunks)]
        + [pltpu.VMEM((positions, kp, SLAB), bf) for _ in range(slabs)]
        + [dma((n_pair, chunks))] * 2
        + [dma((n_sub, chunks))] * 2
        + [dma((n_sub, slabs, 2))] * 2
        + [dma((n_pair, slabs))] * 2,
        compiler_params=pltpu.CompilerParams(
            collective_id=0, has_side_effects=True, vmem_limit_bytes=56 * 1024 * 1024
        ),
        name="exchange",
    )(index, features, w_qk, w_value)

    return pl.pallas_call(
        functools.partial(update_kernel, (sources, slabs)),
        grid=(img_grp,),
        out_shape=jax.ShapeDtypeStruct(features.shape, bf),
        in_specs=[
            smem,
            pl.BlockSpec((None, kp, width), lambda i: (i, 0, 0)),
            vmem,
            vmem,
            vmem,
            vmem,
        ],
        out_specs=pl.BlockSpec((None, kp, width), lambda i: (i, 0, 0)),
        name="update",
    )(weights, features, home, w_out, w_merge_in, w_merge_out)


def solution(mesh):
    in_specs = (
        P(("parts", "pair"), "sub", None),
        P("parts"),
        P("parts", None, None),
        P(),
        P(),
        P(),
        P(),
        P(),
    )
    out_specs = P(("parts", "pair"), "sub", None)
    return jax.shard_map(local, mesh=mesh, in_specs=in_specs, out_specs=out_specs, check_vma=False)
```

```python
import functools

import jax
import jax.numpy as jnp
from jax import lax
from jax.experimental import pallas as pl
from jax.experimental.pallas import tpu as pltpu
from jax.sharding import PartitionSpec as P

HEADS = 4
SLAB = 128
UNITS = 4
MESH = pl.DeviceIdType.MESH

ln_eps = 1e-05


def partner(me, step, n):
    if n & (n - 1):
        return lax.rem(me + step, n)
    peer = 0
    bit = 1
    while bit < n:
        mine = (me // bit) % 2
        peer = peer + ((mine + (step // bit) % 2) % 2) * bit
        bit *= 2
    return peer


def erf(x):
    x = jnp.clip(x, -3.832506856900711, 3.832506856900711)
    y = x * x
    top = jnp.float32(0.00022905065861350646)
    for c in (0.0034082910107109506, 0.050955695062380861, 0.18520832239976145, 1.128379143519084):
        top = top * y + jnp.float32(c)
    low = jnp.float32(-1.1791602954361697e-7)
    for c in (
        0.000023547966471313185,
        0.0010179625278914885,
        0.014070470171167667,
        0.11098505178285362,
        0.49746925110067538,
        1.0,
    ):
        low = low * y + jnp.float32(c)
    return x * top / low


def layer_kernel(
    dims,
    table_ref,
    counts_ref,
    feat_ref,
    wqk_ref,
    wv_ref,
    wout_ref,
    wmi_ref,
    wmo_ref,
    out_ref,
    *scratch,
):
    n_pair, n_sub, per_src, units, slabs, head_dim = dims
    img_grp, kp, width = feat_ref.shape
    positions = 2 * n_sub
    sources = n_pair * per_src
    points = n_sub * kp
    part = kp // units
    tile = n_sub * part
    scratch = list(scratch)
    take, pick, back, share = [scratch.pop(0) for _ in range(4)]
    send1, send2, qk, vx, msg, hsend, mean, hidden, active = [scratch.pop(0) for _ in range(9)]
    arrived = [scratch.pop(0) for _ in range(units)]
    rows_in = [scratch.pop(0) for _ in range(units)]
    returned = [scratch.pop(0) for _ in range(units)]
    home = [scratch.pop(0) for _ in range(units)]
    s1, r1, s2, r2, s3, r3, s4, r4 = scratch

    me_pair = lax.axis_index("pair")
    me_sub = lax.axis_index("sub")

    barrier = pltpu.get_barrier_semaphore()
    for step in range(1, n_pair):
        pl.semaphore_signal(
            barrier, inc=1, device_id={"pair": partner(me_pair, step, n_pair)}, device_id_type=MESH
        )
    for step in range(1, n_sub):
        pl.semaphore_signal(
            barrier, inc=1, device_id={"sub": partner(me_sub, step, n_sub)}, device_id_type=MESH
        )

    low_image = me_pair * img_grp
    zero = jnp.int32(0)

    def owner_tables(owner, uses):
        seen = zero
        chosen = [zero] * per_src
        for j in range(positions):
            image = table_ref[owner * positions + j] - low_image
            here = (image >= 0) & (image < img_grp)
            for r in range(per_src):
                chosen[r] = jnp.where(here & (seen == r), image, chosen[r])
            seen = seen + here.astype(jnp.int32)
        uses = list(uses)
        for r in range(per_src):
            take[owner * per_src + r] = chosen[r]
            for i in range(img_grp):
                hit = ((chosen[r] == i) & (seen > r)).astype(jnp.int32)
                share[i * sources + owner * per_src + r] = hit.astype(jnp.float32)
                uses[i] = uses[i] + hit
        return tuple(uses)

    uses = lax.fori_loop(0, n_pair, owner_tables, (zero,) * img_grp)
    divisor = [jnp.maximum(u, 1).astype(jnp.float32) for u in uses]

    for j in range(positions):
        pick[j] = zero

    def pick_tables(group, carry):
        seen = zero
        chosen = [zero] * per_src
        for j in range(positions):
            image = table_ref[me_pair * positions + j] - group * img_grp
            here = (image >= 0) & (image < img_grp)
            for r in range(per_src):
                chosen[r] = jnp.where(here & (seen == r), j, chosen[r])
            rank = jnp.minimum(seen, per_src - 1)
            pick[j] = jnp.where(here, group * per_src + rank, pick[j])
            seen = seen + here.astype(jnp.int32)
        for r in range(per_src):
            back[group * per_src + r] = chosen[r]
        return carry

    lax.fori_loop(0, n_pair, pick_tables, 0)
    slot_counts = [
        counts_ref[jnp.maximum(table_ref[me_pair * positions + 2 * me_sub + side], 0)]
        for side in range(2)
    ]

    pl.semaphore_wait(barrier, n_pair + n_sub - 2)

    waits = []
    pair_steps = list(range(n_pair - 1, 0, -1))
    sub_steps = list(range(n_sub - 1, 0, -1))

    def send(src, dst, send_sem, recv_sem, device):
        copy = pltpu.make_async_remote_copy(
            src_ref=src,
            dst_ref=dst,
            send_sem=send_sem,
            recv_sem=recv_sem,
            device_id=device,
            device_id_type=MESH,
        )
        copy.start()
        waits.append(copy)
        return copy

    phase1, phase2, phase3, phase4 = {}, {}, {}, {}
    mine1 = pl.ds(me_pair * per_src, per_src)
    for u in range(units):
        rows = pl.ds(u * part, part)
        for step in pair_steps:
            peer = partner(me_pair, step, n_pair)
            for r in range(per_src):
                send1[u, step, r] = feat_ref[take[peer * per_src + r], rows, :]
            phase1[u, step] = send(
                send1.at[u, step], arrived[u].at[mine1], s1.at[step, u], r1.at[step, u], {"pair": peer}
            )
    for u in range(units):
        rows = pl.ds(u * part, part)
        for r in range(per_src):
            own = me_pair * per_src + r
            arrived[u][own] = feat_ref[take[own], rows, :]

    for u in range(units):
        for step in pair_steps:
            phase1[u, step].wait_recv()
        for step in sub_steps:
            peer = partner(me_sub, step, n_sub)
            for side in range(2):
                send2[u, step, side] = arrived[u][pick[2 * peer + side]]
            phase2[u, step] = send(
                send2.at[u, step],
                rows_in[u].at[:, me_sub],
                s2.at[step, u],
                r2.at[step, u],
                {"sub": peer},
            )
        for side in range(2):
            rows_in[u][side, me_sub] = arrived[u][pick[2 * me_sub + side]]

    ones = jnp.ones((tile, SLAB), jnp.bfloat16)
    scale = head_dim ** (-0.5)
    in_slab = SLAB // head_dim
    tile_lane = lax.broadcasted_iota(jnp.int32, (tile, SLAB), 1) // head_dim

    for u in range(units):
        for step in sub_steps:
            phase2[u, step].wait_recv()
        where = pl.ds(u * tile, tile)
        for side in range(2):
            x = rows_in[u][side].reshape(tile, width)
            q = jnp.dot(x, wqk_ref[...], preferred_element_type=jnp.float32)
            qk[side, where, :] = q.astype(jnp.bfloat16)
            v = jnp.dot(x, wv_ref[...], preferred_element_type=jnp.float32).astype(jnp.bfloat16)
            for slab in range(slabs):
                vx[side, slab, where, :SLAB] = v[:, slab * SLAB : (slab + 1) * SLAB]
                vx[side, slab, where, SLAB:] = ones

    order = lax.broadcasted_iota(jnp.int32, (1, points), 1)
    col_ids = (order // part) % n_sub * kp + order // tile * part + order % part

    def attend(u, side):
        other = 1 - side
        valid = col_ids < slot_counts[other]
        for slab in range(slabs):
            columns = slice(slab * SLAB, (slab + 1) * SLAB)
            q = qk[side, pl.ds(u * tile, tile), columns] * jnp.asarray(scale, jnp.bfloat16)
            out = jnp.zeros((tile, SLAB), jnp.float32)
            for head in range(in_slab):
                mine = tile_lane == head
                qh = jnp.where(mine, q, jnp.zeros_like(q))
                sim = lax.dot_general(
                    qh,
                    qk[other, :, columns],
                    (((1,), (1,)), ((), ())),
                    preferred_element_type=jnp.float32,
                )
                sim = jnp.where(valid, sim, -jnp.inf)
                top = jnp.max(sim, axis=1, keepdims=True)
                weight = jnp.exp(sim - top).astype(jnp.bfloat16)
                both = jnp.dot(weight, vx[other, slab], preferred_element_type=jnp.float32)
                out = jnp.where(mine, both[:, :SLAB] / both[:, SLAB:], out)
            msg[u, side, :, :, columns] = out.astype(jnp.bfloat16).reshape(n_sub, part, SLAB)

    def give_back(u, side):
        for step in sub_steps:
            peer = partner(me_sub, step, n_sub)
            phase3[u, side, step] = send(
                msg.at[u, side, peer],
                returned[u].at[2 * me_sub + side],
                s3.at[step, u, side],
                r3.at[step, u, side],
                {"sub": peer},
            )
        returned[u][2 * me_sub + side] = msg[u, side, me_sub]

    def send_home(u):
        for side in range(2):
            for step in sub_steps:
                phase3[u, side, step].wait_recv()
        for step in pair_steps:
            peer = partner(me_pair, step, n_pair)
            for r in range(per_src):
                hsend[u, step, r] = returned[u][back[peer * per_src + r]]
            phase4[u, step] = send(
                hsend.at[u, step], home[u].at[mine1], s4.at[step, u], r4.at[step, u], {"pair": peer}
            )
        for r in range(per_src):
            own = me_pair * per_src + r
            home[u][own] = returned[u][back[own]]

    block = img_grp * part
    strip = 32 if block % 32 == 0 else 16

    def update(u):
        for step in pair_steps:
            phase4[u, step].wait_recv()
        for i in range(img_grp):
            total = jnp.zeros((part, width), jnp.float32)
            for s in range(sources):
                total = total + home[u][s].astype(jnp.float32) * share[i * sources + s]
            mean[pl.ds(i * part, part), :] = (total / divisor[i]).astype(jnp.bfloat16)
        lifted = jnp.dot(mean[...], wout_ref[...], preferred_element_type=jnp.float32)
        feat = feat_ref[:, pl.ds(u * part, part), :].reshape(block, width)
        hidden[...] = jnp.dot(
            feat, wmi_ref[:width, :], preferred_element_type=jnp.float32
        ) + jnp.dot(
            lifted.astype(jnp.bfloat16), wmi_ref[width:, :], preferred_element_type=jnp.float32
        )

        def strip_body(t, carry):
            rows = pl.ds(pl.multiple_of(t * strip, strip), strip)
            h = hidden[rows, :]
            centered = h - jnp.mean(h, axis=-1, keepdims=True)
            variance = jnp.mean(centered * centered, axis=-1, keepdims=True)
            normed = centered * lax.rsqrt(variance + ln_eps)
            gelu = 0.5 * normed * (1.0 + erf(normed * (0.5**0.5)))
            active[rows, :] = gelu.astype(jnp.bfloat16)
            return carry

        lax.fori_loop(0, block // strip, strip_body, 0, unroll=2)
        out = feat.astype(jnp.float32) + jnp.dot(
            active[...], wmo_ref[...], preferred_element_type=jnp.float32
        )
        out_ref[:, pl.ds(u * part, part), :] = out.astype(jnp.bfloat16).reshape(
            img_grp, part, width
        )

    lag = 2
    for u in range(units + lag + 1):
        if u < units:
            for side in range(2):
                attend(u, side)
                give_back(u, side)
        if 0 <= u - lag < units:
            send_home(u - lag)
        if 0 <= u - lag - 1 < units:
            update(u - lag - 1)
    for copy in waits:
        copy.wait_send()


def local(features, counts, pair_table, w_qk, w_value, w_out, w_merge_in, w_merge_out):
    n_pair = lax.axis_size("pair")
    n_sub = lax.axis_size("sub")
    img_grp, kp, width = features.shape
    hidden_width = w_merge_in.shape[1]
    per_src = 2 * n_sub // n_pair
    positions = 2 * n_sub
    sources = n_pair * per_src
    slabs = width // SLAB
    points = n_sub * kp
    units = UNITS
    part = kp // units
    bf = jnp.bfloat16
    dma = pltpu.SemaphoreType.DMA
    vmem = pl.BlockSpec(memory_space=pltpu.VMEM)
    smem = pl.BlockSpec(memory_space=pltpu.SMEM)
    dims = (n_pair, n_sub, per_src, units, slabs, width // HEADS)
    return pl.pallas_call(
        functools.partial(layer_kernel, dims),
        out_shape=jax.ShapeDtypeStruct(features.shape, bf),
        in_specs=[smem, smem] + [vmem] * 6,
        out_specs=vmem,
        scratch_shapes=[
            pltpu.SMEM((sources,), jnp.int32),
            pltpu.SMEM((positions,), jnp.int32),
            pltpu.SMEM((sources,), jnp.int32),
            pltpu.SMEM((img_grp * sources,), jnp.float32),
            pltpu.VMEM((units, n_pair, per_src, part, width), bf),
            pltpu.VMEM((units, n_sub, 2, part, width), bf),
            pltpu.VMEM((2, points, width), bf),
            pltpu.VMEM((2, slabs, points, 2 * SLAB), bf),
            pltpu.VMEM((units, 2, n_sub, part, width), bf),
            pltpu.VMEM((units, n_pair, per_src, part, width), bf),
            pltpu.VMEM((img_grp * part, width), bf),
            pltpu.VMEM((img_grp * part, hidden_width), jnp.float32),
            pltpu.VMEM((img_grp * part, hidden_width), bf),
        ]
        + [pltpu.VMEM((sources, part, width), bf) for _ in range(units)]
        + [pltpu.VMEM((2, n_sub, part, width), bf) for _ in range(units)]
        + [pltpu.VMEM((positions, part, width), bf) for _ in range(units)]
        + [pltpu.VMEM((sources, part, width), bf) for _ in range(units)]
        + [dma((n_pair, units))] * 2
        + [dma((n_sub, units))] * 2
        + [dma((n_sub, units, 2))] * 2
        + [dma((n_pair, units))] * 2,
        compiler_params=pltpu.CompilerParams(
            collective_id=0, has_side_effects=True, vmem_limit_bytes=56 * 1024 * 1024
        ),
        name="layer",
    )(
        pair_table.reshape(-1),
        counts,
        features,
        w_qk,
        w_value,
        w_out,
        w_merge_in,
        w_merge_out,
    )


def solution(mesh):
    in_specs = (
        P(("parts", "pair"), "sub", None),
        P("parts"),
        P("parts", None, None),
        P(),
        P(),
        P(),
        P(),
        P(),
    )
    out_specs = P(("parts", "pair"), "sub", None)
    return jax.shard_map(local, mesh=mesh, in_specs=in_specs, out_specs=out_specs, check_vma=False)
```

```python
import functools

import jax
import jax.numpy as jnp
from jax import lax
from jax.experimental import pallas as pl
from jax.experimental.pallas import tpu as pltpu
from jax.sharding import PartitionSpec as P

HEADS = 4
SLAB = 128
UNITS = 4
MESH = pl.DeviceIdType.MESH

ln_eps = 1e-05


def partner(me, step, n):
    if n & (n - 1):
        return lax.rem(me + step, n)
    peer = 0
    bit = 1
    while bit < n:
        mine = (me // bit) % 2
        peer = peer + ((mine + (step // bit) % 2) % 2) * bit
        bit *= 2
    return peer


def erf(x):
    x = jnp.clip(x, -3.832506856900711, 3.832506856900711)
    y = x * x
    top = jnp.float32(0.00022905065861350646)
    for c in (0.0034082910107109506, 0.050955695062380861, 0.18520832239976145, 1.128379143519084):
        top = top * y + jnp.float32(c)
    low = jnp.float32(-1.1791602954361697e-7)
    for c in (
        0.000023547966471313185,
        0.0010179625278914885,
        0.014070470171167667,
        0.11098505178285362,
        0.49746925110067538,
        1.0,
    ):
        low = low * y + jnp.float32(c)
    return x * top / low


def layer_kernel(
    dims,
    table_ref,
    counts_ref,
    feat_ref,
    wqk_hbm,
    wv_hbm,
    wout_hbm,
    wmi_hbm,
    wmo_hbm,
    out_ref,
    *scratch,
):
    n_pair, n_sub, per_src, units, slabs, head_dim = dims
    img_grp, kp, width = feat_ref.shape
    positions = 2 * n_sub
    sources = n_pair * per_src
    points = n_sub * kp
    part = kp // units
    tile = n_sub * part
    scratch = list(scratch)
    take, held, pick, back, share = [scratch.pop(0) for _ in range(5)]
    send1, send2, qk, vx, msg, hsend, mean, hidden, active = [scratch.pop(0) for _ in range(9)]
    wqk_ref, wv_ref, wout_ref, wmi_ref, wmo_ref, wsem = [scratch.pop(0) for _ in range(6)]
    arrived = [scratch.pop(0) for _ in range(units)]
    rows_in = [scratch.pop(0) for _ in range(units)]
    returned = [scratch.pop(0) for _ in range(units)]
    home = [scratch.pop(0) for _ in range(units)]
    s1, r1, s2, r2, s3, r3, s4, r4 = scratch

    me_pair = lax.axis_index("pair")
    me_sub = lax.axis_index("sub")

    weights = [
        pltpu.make_async_copy(src, dst, wsem.at[n])
        for n, (src, dst) in enumerate(
            (
                (wqk_hbm, wqk_ref),
                (wv_hbm, wv_ref),
                (wout_hbm, wout_ref),
                (wmi_hbm, wmi_ref),
                (wmo_hbm, wmo_ref),
            )
        )
    ]
    barrier = pltpu.get_barrier_semaphore()
    for step in range(1, n_pair):
        pl.semaphore_signal(
            barrier, inc=1, device_id={"pair": partner(me_pair, step, n_pair)}, device_id_type=MESH
        )
    for step in range(1, n_sub):
        pl.semaphore_signal(
            barrier, inc=1, device_id={"sub": partner(me_sub, step, n_sub)}, device_id_type=MESH
        )

    low_image = me_pair * img_grp
    zero = jnp.int32(0)

    def send_table(owner, carry):
        seen = zero
        chosen = [zero] * per_src
        for j in range(positions):
            image = table_ref[owner, j // 2, j % 2] - low_image
            here = (image >= 0) & (image < img_grp)
            for r in range(per_src):
                chosen[r] = jnp.where(here & (seen == r), image, chosen[r])
            seen = seen + here.astype(jnp.int32)
        for r in range(per_src):
            take[owner * per_src + r] = chosen[r]
            held[owner * per_src + r] = jnp.where(seen > r, chosen[r], -1)
        return carry

    lax.fori_loop(0, n_pair, send_table, 0)
    pl.semaphore_wait(barrier, n_pair + n_sub - 2)
    for copy in weights:
        copy.start()
    waits = []
    pair_steps = list(range(n_pair - 1, 0, -1))
    sub_steps = list(range(n_sub - 1, 0, -1))

    def send(src, dst, send_sem, recv_sem, device):
        copy = pltpu.make_async_remote_copy(
            src_ref=src,
            dst_ref=dst,
            send_sem=send_sem,
            recv_sem=recv_sem,
            device_id=device,
            device_id_type=MESH,
        )
        copy.start()
        waits.append(copy)
        return copy

    phase1, phase2, phase3, phase4 = {}, {}, {}, {}
    mine1 = pl.ds(me_pair * per_src, per_src)
    for u in range(units):
        rows = pl.ds(u * part, part)
        for step in pair_steps:
            peer = partner(me_pair, step, n_pair)
            for r in range(per_src):
                send1[u, step, r] = feat_ref[take[peer * per_src + r], rows, :]
            phase1[u, step] = send(
                send1.at[u, step], arrived[u].at[mine1], s1.at[step, u], r1.at[step, u], {"pair": peer}
            )
    for u in range(units):
        rows = pl.ds(u * part, part)
        for r in range(per_src):
            own = me_pair * per_src + r
            arrived[u][own] = feat_ref[take[own], rows, :]

    for j in range(positions):
        pick[j] = zero

    def pick_tables(group, carry):
        seen = zero
        chosen = [zero] * per_src
        for j in range(positions):
            image = table_ref[me_pair, j // 2, j % 2] - group * img_grp
            here = (image >= 0) & (image < img_grp)
            for r in range(per_src):
                chosen[r] = jnp.where(here & (seen == r), j, chosen[r])
            rank = jnp.minimum(seen, per_src - 1)
            pick[j] = jnp.where(here, group * per_src + rank, pick[j])
            seen = seen + here.astype(jnp.int32)
        for r in range(per_src):
            back[group * per_src + r] = chosen[r]
        return carry

    lax.fori_loop(0, n_pair, pick_tables, 0)
    slot_counts = [
        counts_ref[jnp.maximum(table_ref[me_pair, me_sub, side], 0)]
        for side in range(2)
    ]

    def share_table(s, uses):
        uses = list(uses)
        for i in range(img_grp):
            hit = (held[s] == i).astype(jnp.int32)
            share[i * sources + s] = hit.astype(jnp.float32)
            uses[i] = uses[i] + hit
        return tuple(uses)

    uses = lax.fori_loop(0, sources, share_table, (zero,) * img_grp)
    divisor = [jnp.maximum(u, 1).astype(jnp.float32) for u in uses]

    for u in range(units):
        for step in pair_steps:
            phase1[u, step].wait_recv()
        for step in sub_steps:
            peer = partner(me_sub, step, n_sub)
            for side in range(2):
                send2[u, step, side] = arrived[u][pick[2 * peer + side]]
            phase2[u, step] = send(
                send2.at[u, step],
                rows_in[u].at[:, me_sub],
                s2.at[step, u],
                r2.at[step, u],
                {"sub": peer},
            )
        for side in range(2):
            rows_in[u][side, me_sub] = arrived[u][pick[2 * me_sub + side]]

    weights[0].wait()
    weights[1].wait()
    ones = jnp.ones((tile, SLAB), jnp.bfloat16)
    scale = head_dim ** (-0.5)
    in_slab = SLAB // head_dim
    tile_lane = lax.broadcasted_iota(jnp.int32, (tile, SLAB), 1) // head_dim

    for u in range(units):
        for step in sub_steps:
            phase2[u, step].wait_recv()
        where = pl.ds(u * tile, tile)
        for side in range(2):
            x = rows_in[u][side].reshape(tile, width)
            q = jnp.dot(x, wqk_ref[...], preferred_element_type=jnp.float32)
            qk[side, where, :] = q.astype(jnp.bfloat16)
            v = jnp.dot(x, wv_ref[...], preferred_element_type=jnp.float32).astype(jnp.bfloat16)
            for slab in range(slabs):
                vx[side, slab, where, :SLAB] = v[:, slab * SLAB : (slab + 1) * SLAB]
                vx[side, slab, where, SLAB:] = ones

    order = lax.broadcasted_iota(jnp.int32, (1, points), 1)
    col_ids = (order // part) % n_sub * kp + order // tile * part + order % part

    def attend(u, side):
        other = 1 - side
        valid = col_ids < slot_counts[other]
        for slab in range(slabs):
            columns = slice(slab * SLAB, (slab + 1) * SLAB)
            q = qk[side, pl.ds(u * tile, tile), columns] * jnp.asarray(scale, jnp.bfloat16)
            out = jnp.zeros((tile, SLAB), jnp.float32)
            for head in range(in_slab):
                mine = tile_lane == head
                qh = jnp.where(mine, q, jnp.zeros_like(q))
                sim = lax.dot_general(
                    qh,
                    qk[other, :, columns],
                    (((1,), (1,)), ((), ())),
                    preferred_element_type=jnp.float32,
                )
                sim = jnp.where(valid, sim, -jnp.inf)
                top = jnp.max(sim, axis=1, keepdims=True)
                weight = jnp.exp(sim - top).astype(jnp.bfloat16)
                both = jnp.dot(weight, vx[other, slab], preferred_element_type=jnp.float32)
                out = jnp.where(mine, both[:, :SLAB] / both[:, SLAB:], out)
            msg[u, side, :, :, columns] = out.astype(jnp.bfloat16).reshape(n_sub, part, SLAB)

    def give_back(u, side):
        for step in sub_steps:
            peer = partner(me_sub, step, n_sub)
            phase3[u, side, step] = send(
                msg.at[u, side, peer],
                returned[u].at[2 * me_sub + side],
                s3.at[step, u, side],
                r3.at[step, u, side],
                {"sub": peer},
            )
        returned[u][2 * me_sub + side] = msg[u, side, me_sub]

    def send_home(u):
        for side in range(2):
            for step in sub_steps:
                phase3[u, side, step].wait_recv()
        for step in pair_steps:
            peer = partner(me_pair, step, n_pair)
            for r in range(per_src):
                hsend[u, step, r] = returned[u][back[peer * per_src + r]]
            phase4[u, step] = send(
                hsend.at[u, step], home[u].at[mine1], s4.at[step, u], r4.at[step, u], {"pair": peer}
            )
        for r in range(per_src):
            own = me_pair * per_src + r
            home[u][own] = returned[u][back[own]]

    block = img_grp * part
    strip = block // 2

    def update(u):
        feat = feat_ref[:, pl.ds(u * part, part), :].reshape(block, width)
        hidden[...] = jnp.dot(feat, wmi_ref[:width, :], preferred_element_type=jnp.float32)
        for step in pair_steps:
            phase4[u, step].wait_recv()
        for i in range(img_grp):
            total = jnp.zeros((part, width), jnp.float32)
            for s in range(sources):
                total = total + home[u][s].astype(jnp.float32) * share[i * sources + s]
            mean[pl.ds(i * part, part), :] = (total / divisor[i]).astype(jnp.bfloat16)
        lifted = jnp.dot(mean[...], wout_ref[...], preferred_element_type=jnp.float32)
        hidden[...] = hidden[...] + jnp.dot(
            lifted.astype(jnp.bfloat16), wmi_ref[width:, :], preferred_element_type=jnp.float32
        )

        def strip_body(t, carry):
            rows = pl.ds(pl.multiple_of(t * strip, strip), strip)
            h = hidden[rows, :]
            centered = h - jnp.mean(h, axis=-1, keepdims=True)
            variance = jnp.mean(centered * centered, axis=-1, keepdims=True)
            normed = centered * lax.rsqrt(variance + ln_eps)
            gelu = 0.5 * normed * (1.0 + erf(normed * (0.5**0.5)))
            active[rows, :] = gelu.astype(jnp.bfloat16)
            return carry

        lax.fori_loop(0, block // strip, strip_body, 0)
        out = feat.astype(jnp.float32) + jnp.dot(
            active[...], wmo_ref[...], preferred_element_type=jnp.float32
        )
        out_ref[:, pl.ds(u * part, part), :] = out.astype(jnp.bfloat16).reshape(
            img_grp, part, width
        )

    for copy in weights[2:]:
        copy.wait()
    lag = 2
    for u in range(units + lag + 1):
        if u < units:
            for side in range(2):
                attend(u, side)
                give_back(u, side)
        if 0 <= u - lag < units:
            send_home(u - lag)
        if 0 <= u - lag - 1 < units:
            update(u - lag - 1)
    for copy in waits:
        copy.wait_send()


def local(features, counts, pair_table, w_qk, w_value, w_out, w_merge_in, w_merge_out):
    n_pair = lax.axis_size("pair")
    n_sub = lax.axis_size("sub")
    img_grp, kp, width = features.shape
    hidden_width = w_merge_in.shape[1]
    per_src = 2 * n_sub // n_pair
    positions = 2 * n_sub
    sources = n_pair * per_src
    slabs = width // SLAB
    points = n_sub * kp
    units = min(UNITS, kp // 16)
    part = kp // units
    bf = jnp.bfloat16
    dma = pltpu.SemaphoreType.DMA
    vmem = pl.BlockSpec(memory_space=pltpu.VMEM)
    smem = pl.BlockSpec(memory_space=pltpu.SMEM)
    dims = (n_pair, n_sub, per_src, units, slabs, width // HEADS)
    return pl.pallas_call(
        functools.partial(layer_kernel, dims),
        out_shape=jax.ShapeDtypeStruct(features.shape, bf),
        in_specs=[smem, smem, vmem] + [pl.BlockSpec(memory_space=pl.ANY)] * 5,
        out_specs=vmem,
        scratch_shapes=[
            pltpu.SMEM((sources,), jnp.int32),
            pltpu.SMEM((sources,), jnp.int32),
            pltpu.SMEM((positions,), jnp.int32),
            pltpu.SMEM((sources,), jnp.int32),
            pltpu.SMEM((img_grp * sources,), jnp.float32),
            pltpu.VMEM((units, n_pair, per_src, part, width), bf),
            pltpu.VMEM((units, n_sub, 2, part, width), bf),
            pltpu.VMEM((2, points, width), bf),
            pltpu.VMEM((2, slabs, points, 2 * SLAB), bf),
            pltpu.VMEM((units, 2, n_sub, part, width), bf),
            pltpu.VMEM((units, n_pair, per_src, part, width), bf),
            pltpu.VMEM((img_grp * part, width), bf),
            pltpu.VMEM((img_grp * part, hidden_width), jnp.float32),
            pltpu.VMEM((img_grp * part, hidden_width), bf),
        ]
        + [pltpu.VMEM(w.shape, bf) for w in (w_qk, w_value, w_out, w_merge_in, w_merge_out)]
        + [
            dma((5,)),
        ]
        + [pltpu.VMEM((sources, part, width), bf) for _ in range(units)]
        + [pltpu.VMEM((2, n_sub, part, width), bf) for _ in range(units)]
        + [pltpu.VMEM((positions, part, width), bf) for _ in range(units)]
        + [pltpu.VMEM((sources, part, width), bf) for _ in range(units)]
        + [dma((n_pair, units))] * 2
        + [dma((n_sub, units))] * 2
        + [dma((n_sub, units, 2))] * 2
        + [dma((n_pair, units))] * 2,
        compiler_params=pltpu.CompilerParams(
            collective_id=0, has_side_effects=True, vmem_limit_bytes=56 * 1024 * 1024
        ),
        name="layer",
    )(
        pair_table,
        counts,
        features,
        w_qk,
        w_value,
        w_out,
        w_merge_in,
        w_merge_out,
    )


def solution(mesh):
    in_specs = (
        P(("parts", "pair"), "sub", None),
        P("parts"),
        P("parts", None, None),
        P(),
        P(),
        P(),
        P(),
        P(),
    )
    out_specs = P(("parts", "pair"), "sub", None)
    return jax.shard_map(local, mesh=mesh, in_specs=in_specs, out_specs=out_specs, check_vma=False)
```

```python
import functools

import jax
import jax.numpy as jnp
from jax import lax
from jax.experimental import pallas as pl
from jax.experimental.pallas import tpu as pltpu
from jax.sharding import PartitionSpec as P

HEADS = 4
SLAB = 128
UNITS = 4
MESH = pl.DeviceIdType.MESH

ln_eps = 1e-05


def partner(me, step, n):
    if n & (n - 1):
        return lax.rem(me + step, n)
    peer = 0
    bit = 1
    while bit < n:
        mine = (me // bit) % 2
        peer = peer + ((mine + (step // bit) % 2) % 2) * bit
        bit *= 2
    return peer


def erf(x):
    x = jnp.clip(x, -3.832506856900711, 3.832506856900711)
    y = x * x
    top = jnp.float32(0.00022905065861350646)
    for c in (0.0034082910107109506, 0.050955695062380861, 0.18520832239976145, 1.128379143519084):
        top = top * y + jnp.float32(c)
    low = jnp.float32(-1.1791602954361697e-7)
    for c in (
        0.000023547966471313185,
        0.0010179625278914885,
        0.014070470171167667,
        0.11098505178285362,
        0.49746925110067538,
        1.0,
    ):
        low = low * y + jnp.float32(c)
    return x * top / low


def layer_kernel(
    dims,
    table_ref,
    counts_ref,
    feat_ref,
    wqk_hbm,
    wv_hbm,
    wout_hbm,
    wmi_hbm,
    wmo_hbm,
    out_ref,
    *scratch,
):
    n_pair, n_sub, per_src, units, slabs, head_dim = dims
    img_grp, kp, width = feat_ref.shape
    positions = 2 * n_sub
    sources = n_pair * per_src
    points = n_sub * kp
    part = kp // units
    tile = n_sub * part
    scratch = list(scratch)
    take, held, pick, back, share = [scratch.pop(0) for _ in range(5)]
    send1, send2, qk, vx, msg, hsend, mean, hidden, active = [scratch.pop(0) for _ in range(9)]
    wqk_ref, wv_ref, wout_ref, wmi_ref, wmo_ref, wsem = [scratch.pop(0) for _ in range(6)]
    arrived = [scratch.pop(0) for _ in range(units)]
    rows_in = [scratch.pop(0) for _ in range(units)]
    returned = [scratch.pop(0) for _ in range(units)]
    home = [scratch.pop(0) for _ in range(units)]
    s1, r1, s2, r2, s3, r3, s4, r4 = scratch

    me_pair = lax.axis_index("pair")
    me_sub = lax.axis_index("sub")

    weights = [
        pltpu.make_async_copy(src, dst, wsem.at[n])
        for n, (src, dst) in enumerate(
            (
                (wqk_hbm, wqk_ref),
                (wv_hbm, wv_ref),
                (wout_hbm, wout_ref),
                (wmi_hbm, wmi_ref),
                (wmo_hbm, wmo_ref),
            )
        )
    ]
    barrier = pltpu.get_barrier_semaphore()
    for step in range(1, n_pair):
        pl.semaphore_signal(
            barrier, inc=1, device_id={"pair": partner(me_pair, step, n_pair)}, device_id_type=MESH
        )
    for step in range(1, n_sub):
        pl.semaphore_signal(
            barrier, inc=1, device_id={"sub": partner(me_sub, step, n_sub)}, device_id_type=MESH
        )

    low_image = me_pair * img_grp
    zero = jnp.int32(0)

    def send_table(owner, carry):
        seen = zero
        chosen = [zero] * per_src
        for j in range(positions):
            image = table_ref[owner, j % 2, j // 2] - low_image
            here = (image >= 0) & (image < img_grp)
            for r in range(per_src):
                chosen[r] = jnp.where(here & (seen == r), image, chosen[r])
            seen = seen + here.astype(jnp.int32)
        for r in range(per_src):
            take[owner * per_src + r] = chosen[r]
            held[owner * per_src + r] = jnp.where(seen > r, chosen[r], -1)
        return carry

    lax.fori_loop(0, n_pair, send_table, 0)
    pl.semaphore_wait(barrier, n_pair + n_sub - 2)
    for copy in weights:
        copy.start()
    waits = []
    pair_steps = list(range(n_pair - 1, 0, -1))
    sub_steps = list(range(n_sub - 1, 0, -1))

    def send(src, dst, send_sem, recv_sem, device):
        copy = pltpu.make_async_remote_copy(
            src_ref=src,
            dst_ref=dst,
            send_sem=send_sem,
            recv_sem=recv_sem,
            device_id=device,
            device_id_type=MESH,
        )
        copy.start()
        waits.append(copy)
        return copy

    phase1, phase2, phase3, phase4 = {}, {}, {}, {}
    mine1 = pl.ds(me_pair * per_src, per_src)
    for u in range(units):
        rows = pl.ds(u * part, part)
        for step in pair_steps:
            peer = partner(me_pair, step, n_pair)
            for r in range(per_src):
                send1[u, step, r] = feat_ref[take[peer * per_src + r], rows, :]
            phase1[u, step] = send(
                send1.at[u, step], arrived[u].at[mine1], s1.at[step, u], r1.at[step, u], {"pair": peer}
            )
    for u in range(units):
        rows = pl.ds(u * part, part)
        for r in range(per_src):
            own = me_pair * per_src + r
            arrived[u][own] = feat_ref[take[own], rows, :]

    for j in range(positions):
        pick[j] = zero

    def pick_tables(group, carry):
        seen = zero
        chosen = [zero] * per_src
        for j in range(positions):
            image = table_ref[me_pair, j % 2, j // 2] - group * img_grp
            here = (image >= 0) & (image < img_grp)
            for r in range(per_src):
                chosen[r] = jnp.where(here & (seen == r), j, chosen[r])
            rank = jnp.minimum(seen, per_src - 1)
            pick[j] = jnp.where(here, group * per_src + rank, pick[j])
            seen = seen + here.astype(jnp.int32)
        for r in range(per_src):
            back[group * per_src + r] = chosen[r]
        return carry

    lax.fori_loop(0, n_pair, pick_tables, 0)
    slot_counts = [
        counts_ref[jnp.maximum(table_ref[me_pair, side, me_sub], 0)]
        for side in range(2)
    ]

    def share_table(s, uses):
        uses = list(uses)
        for i in range(img_grp):
            hit = (held[s] == i).astype(jnp.int32)
            share[i * sources + s] = hit.astype(jnp.float32)
            uses[i] = uses[i] + hit
        return tuple(uses)

    uses = lax.fori_loop(0, sources, share_table, (zero,) * img_grp)
    divisor = [jnp.maximum(u, 1).astype(jnp.float32) for u in uses]

    for u in range(units):
        for step in pair_steps:
            phase1[u, step].wait_recv()
        for step in sub_steps:
            peer = partner(me_sub, step, n_sub)
            for side in range(2):
                send2[u, step, side] = arrived[u][pick[2 * peer + side]]
            phase2[u, step] = send(
                send2.at[u, step],
                rows_in[u].at[:, me_sub],
                s2.at[step, u],
                r2.at[step, u],
                {"sub": peer},
            )
        for side in range(2):
            rows_in[u][side, me_sub] = arrived[u][pick[2 * me_sub + side]]

    weights[0].wait()
    weights[1].wait()
    ones = jnp.ones((tile, SLAB), jnp.bfloat16)
    scale = head_dim ** (-0.5)
    in_slab = SLAB // head_dim
    tile_lane = lax.broadcasted_iota(jnp.int32, (tile, SLAB), 1) // head_dim

    for u in range(units):
        for step in sub_steps:
            phase2[u, step].wait_recv()
        where = pl.ds(u * tile, tile)
        for side in range(2):
            x = rows_in[u][side].reshape(tile, width)
            q = jnp.dot(x, wqk_ref[...], preferred_element_type=jnp.float32)
            qk[side, where, :] = q.astype(jnp.bfloat16)
            v = jnp.dot(x, wv_ref[...], preferred_element_type=jnp.float32).astype(jnp.bfloat16)
            for slab in range(slabs):
                vx[side, slab, where, :SLAB] = v[:, slab * SLAB : (slab + 1) * SLAB]
                vx[side, slab, where, SLAB:] = ones

    order = lax.broadcasted_iota(jnp.int32, (1, points), 1)
    col_ids = (order // part) % n_sub * kp + order // tile * part + order % part

    def attend(u, side):
        other = 1 - side
        valid = col_ids < slot_counts[other]
        for slab in range(slabs):
            columns = slice(slab * SLAB, (slab + 1) * SLAB)
            q = qk[side, pl.ds(u * tile, tile), columns] * jnp.asarray(scale, jnp.bfloat16)
            out = jnp.zeros((tile, SLAB), jnp.float32)
            for head in range(in_slab):
                mine = tile_lane == head
                qh = jnp.where(mine, q, jnp.zeros_like(q))
                sim = lax.dot_general(
                    qh,
                    qk[other, :, columns],
                    (((1,), (1,)), ((), ())),
                    preferred_element_type=jnp.float32,
                )
                sim = jnp.where(valid, sim, -jnp.inf)
                top = jnp.max(sim, axis=1, keepdims=True)
                weight = jnp.exp(sim - top).astype(jnp.bfloat16)
                both = jnp.dot(weight, vx[other, slab], preferred_element_type=jnp.float32)
                out = jnp.where(mine, both[:, :SLAB] / both[:, SLAB:], out)
            msg[u, side, :, :, columns] = out.astype(jnp.bfloat16).reshape(n_sub, part, SLAB)

    def give_back(u, side):
        for step in sub_steps:
            peer = partner(me_sub, step, n_sub)
            phase3[u, side, step] = send(
                msg.at[u, side, peer],
                returned[u].at[2 * me_sub + side],
                s3.at[step, u, side],
                r3.at[step, u, side],
                {"sub": peer},
            )
        returned[u][2 * me_sub + side] = msg[u, side, me_sub]

    def send_home(u):
        for side in range(2):
            for step in sub_steps:
                phase3[u, side, step].wait_recv()
        for step in pair_steps:
            peer = partner(me_pair, step, n_pair)
            for r in range(per_src):
                hsend[u, step, r] = returned[u][back[peer * per_src + r]]
            phase4[u, step] = send(
                hsend.at[u, step], home[u].at[mine1], s4.at[step, u], r4.at[step, u], {"pair": peer}
            )
        for r in range(per_src):
            own = me_pair * per_src + r
            home[u][own] = returned[u][back[own]]

    block = img_grp * part
    strip = block // 2

    def update(u):
        feat = feat_ref[:, pl.ds(u * part, part), :].reshape(block, width)
        hidden[...] = jnp.dot(feat, wmi_ref[:width, :], preferred_element_type=jnp.float32)
        for step in pair_steps:
            phase4[u, step].wait_recv()
        for i in range(img_grp):
            total = jnp.zeros((part, width), jnp.float32)
            for s in range(sources):
                total = total + home[u][s].astype(jnp.float32) * share[i * sources + s]
            mean[pl.ds(i * part, part), :] = (total / divisor[i]).astype(jnp.bfloat16)
        lifted = jnp.dot(mean[...], wout_ref[...], preferred_element_type=jnp.float32)
        hidden[...] = hidden[...] + jnp.dot(
            lifted.astype(jnp.bfloat16), wmi_ref[width:, :], preferred_element_type=jnp.float32
        )

        def strip_body(t, carry):
            rows = pl.ds(pl.multiple_of(t * strip, strip), strip)
            h = hidden[rows, :]
            centered = h - jnp.mean(h, axis=-1, keepdims=True)
            variance = jnp.mean(centered * centered, axis=-1, keepdims=True)
            normed = centered * lax.rsqrt(variance + ln_eps)
            gelu = 0.5 * normed * (1.0 + erf(normed * (0.5**0.5)))
            active[rows, :] = gelu.astype(jnp.bfloat16)
            return carry

        lax.fori_loop(0, block // strip, strip_body, 0)
        out = feat.astype(jnp.float32) + jnp.dot(
            active[...], wmo_ref[...], preferred_element_type=jnp.float32
        )
        out_ref[:, pl.ds(u * part, part), :] = out.astype(jnp.bfloat16).reshape(
            img_grp, part, width
        )

    for copy in weights[2:]:
        copy.wait()
    lag = 2
    for u in range(units + lag + 1):
        if u < units:
            for side in range(2):
                attend(u, side)
                give_back(u, side)
        if 0 <= u - lag < units:
            send_home(u - lag)
        if 0 <= u - lag - 1 < units:
            update(u - lag - 1)
    for copy in waits:
        copy.wait_send()


def local(features, counts, pair_table, w_qk, w_value, w_out, w_merge_in, w_merge_out):
    n_pair = lax.axis_size("pair")
    n_sub = lax.axis_size("sub")
    img_grp, kp, width = features.shape
    hidden_width = w_merge_in.shape[1]
    per_src = 2 * n_sub // n_pair
    positions = 2 * n_sub
    sources = n_pair * per_src
    slabs = width // SLAB
    points = n_sub * kp
    units = min(UNITS, kp // 16)
    part = kp // units
    bf = jnp.bfloat16
    dma = pltpu.SemaphoreType.DMA
    vmem = pl.BlockSpec(memory_space=pltpu.VMEM)
    smem = pl.BlockSpec(memory_space=pltpu.SMEM)
    dims = (n_pair, n_sub, per_src, units, slabs, width // HEADS)
    return pl.pallas_call(
        functools.partial(layer_kernel, dims),
        out_shape=jax.ShapeDtypeStruct(features.shape, bf),
        in_specs=[smem, smem, vmem] + [pl.BlockSpec(memory_space=pl.ANY)] * 5,
        out_specs=vmem,
        scratch_shapes=[
            pltpu.SMEM((sources,), jnp.int32),
            pltpu.SMEM((sources,), jnp.int32),
            pltpu.SMEM((positions,), jnp.int32),
            pltpu.SMEM((sources,), jnp.int32),
            pltpu.SMEM((img_grp * sources,), jnp.float32),
            pltpu.VMEM((units, n_pair, per_src, part, width), bf),
            pltpu.VMEM((units, n_sub, 2, part, width), bf),
            pltpu.VMEM((2, points, width), bf),
            pltpu.VMEM((2, slabs, points, 2 * SLAB), bf),
            pltpu.VMEM((units, 2, n_sub, part, width), bf),
            pltpu.VMEM((units, n_pair, per_src, part, width), bf),
            pltpu.VMEM((img_grp * part, width), bf),
            pltpu.VMEM((img_grp * part, hidden_width), jnp.float32),
            pltpu.VMEM((img_grp * part, hidden_width), bf),
        ]
        + [pltpu.VMEM(w.shape, bf) for w in (w_qk, w_value, w_out, w_merge_in, w_merge_out)]
        + [
            dma((5,)),
        ]
        + [pltpu.VMEM((sources, part, width), bf) for _ in range(units)]
        + [pltpu.VMEM((2, n_sub, part, width), bf) for _ in range(units)]
        + [pltpu.VMEM((positions, part, width), bf) for _ in range(units)]
        + [pltpu.VMEM((sources, part, width), bf) for _ in range(units)]
        + [dma((n_pair, units))] * 2
        + [dma((n_sub, units))] * 2
        + [dma((n_sub, units, 2))] * 2
        + [dma((n_pair, units))] * 2,
        compiler_params=pltpu.CompilerParams(
            collective_id=0, has_side_effects=True, vmem_limit_bytes=56 * 1024 * 1024
        ),
        name="layer",
    )(
        jnp.swapaxes(pair_table, 1, 2),
        counts,
        features,
        w_qk,
        w_value,
        w_out,
        w_merge_in,
        w_merge_out,
    )


def solution(mesh):
    in_specs = (
        P(("parts", "pair"), "sub", None),
        P("parts"),
        P("parts", None, None),
        P(),
        P(),
        P(),
        P(),
        P(),
    )
    out_specs = P(("parts", "pair"), "sub", None)
    return jax.shard_map(local, mesh=mesh, in_specs=in_specs, out_specs=out_specs, check_vma=False)
```
